32 devices in a mesh: blk: 8 (over z, x), road: 4 (over y, core).
Axes of the slice: x: 2, y: 2, z: 4, core: 2. Of those that a mesh axis runs over, the one named last changes fastest.
Arguments:
- disp: float32 [3, 16, 64, 1024], P(None, None, 'road', 'blk'), may hold values from -1.2 to 1.2
- veloc: float32 [3, 16, 64, 1024], P(None, None, 'road', 'blk'), may hold values from -6 to 6
- stiff: float32 [3, 16, 64, 1024], P(None, None, 'road', 'blk'), may hold values from 0.5 to 2
- mass: float32 [16, 64, 1024], P(None, 'road', 'blk'), may hold values from 1 to 4
- road_height: float32 [16384], P('road'), may hold values from -1.2 to 1.2
- road_slope_x: float32 [16384], P('road'), may hold values from -0.3 to 0.3
- road_slope_y: float32 [16384], P('road'), may hold values from -0.3 to 0.3
- road_stiff: float32 [16384], P('road'), may hold values from 1 to 4
- tile_list: int32 [8, 4, 4], P('blk', 'road'), may hold values from 0 to 63, as said below
- pair_node: int32 [8, 4, 8192], P('blk', 'road'), may hold values from 0 to 2047, as said below
- pair_slot: int32 [8, 4, 8192], P('blk', 'road'), may hold values from 0 to 1023, as said below
- pair_count: int32 [8, 4], P('blk', 'road'), may hold values from 0 to 8192, as said below
Outputs:
- veloc_out: float32 [3, 16, 64, 1024], P(None, None, 'road', 'blk')
- road_load: float32 [16384], P(('blk', 'road'))
The draws below stay inside these ranges and needn't reach their ends.
Inputs may be any that keep to these rules, and one draw needn't show every extreme that they name: `pair_count`: the sectors with live slots form one run of 1 consecutive sectors round the cycle, possibly across its end; on their devices from 4096 to 8192 slots are live, and some device has all 8192 live; on all other devices none. Index of a node of the device's own outer layer: lateral position pair_node // 128, circumferential position pair_node % 128 within the device's block. Position within the device's listed tiles: tile pair_slot // 256, facet pair_slot % 256 of that tile. `tile_list`: 4 consecutive tile numbers counted modulo 64; tile t holds facets t * 256 to t * 256 + 255, on road patch t // 16.
All inputs are finite; a program needn't handle non-finite values.
Results may differ from the reference program's by a relative error of at most 0.0001.
Values sent between devices are 32-bit elements; how exact they have to be, the bound alone decides.
A program may use at most 64 MiB of HBM per device.

```python
import math
import jax
import jax.numpy as jnp
from jax import lax

NR = 16
NL = 16
NC = 128
PAIRS = 8192
TILE = 256
TILES_NEED = 4
STEPS = 2
SECTORS = 8
BANDS = 4
CONTACT = 1
FACETS = 16384
TOTAL_TILES = 64
NLT = 64
NCT = 1024


def draw_pair_count(key, part):
    first = jax.random.randint(jax.random.fold_in(key, 11), (), 0, SECTORS)
    sector = jnp.arange(SECTORS, dtype=jnp.int32)
    touching = (sector - first) % SECTORS < CONTACT
    drawn = jax.random.randint(jax.random.fold_in(key, 12), (SECTORS, BANDS), PAIRS // 2, PAIRS + 1).astype(jnp.int32)
    drawn = drawn.at[first, 0].set(PAIRS)
    counts = jnp.where(touching[:, None], drawn, 0)
    return counts.astype(jnp.int32)


def draw_pair_node(key, part):
    drawn = jax.random.randint(jax.random.fold_in(key, 21), (SECTORS, BANDS, PAIRS), 0, NL * NC).astype(jnp.int32)
    return drawn.at[0, 0, 0].set(NL * NC - 1).at[0, 0, 1].set(0)


def draw_pair_slot(key, part):
    drawn = jax.random.randint(jax.random.fold_in(key, 31), (SECTORS, BANDS, PAIRS), 0, TILES_NEED * TILE).astype(jnp.int32)
    return drawn.at[0, 0, 0].set(TILES_NEED * TILE - 1).at[0, 0, 1].set(0)


def draw_tile_list(key, part):
    offsets = jax.random.randint(jax.random.fold_in(key, 41), (SECTORS, BANDS), 0, TOTAL_TILES).astype(jnp.int32)
    offsets = offsets.at[0, 0].set(TOTAL_TILES - 1)
    steps_along = jnp.arange(TILES_NEED, dtype=jnp.int32)
    return ((offsets[:, :, None] + steps_along[None, None, :]) % TOTAL_TILES).astype(jnp.int32)


def level_of(rng, dims, cuts, least, top_value):
    level = 1.0
    for position, blocks in cuts:
        draws = jax.random.uniform(jax.random.fold_in(jax.random.fold_in(rng, 6), position), (blocks,), jnp.float32, least / len(cuts), top_value / len(cuts))
        level = level * jnp.repeat(jnp.exp(draws), dims[position] // blocks).reshape((-1,) + (1,) * (len(dims) - 1 - position))
    return level


def centred(key, dims, scale, limit, cuts=(), kind=jnp.bfloat16):
    array = jax.random.normal(key, dims, jnp.float32) * scale
    if len(cuts) > 0:
        array = level_of(key, dims, cuts, -0.22, 0.18) * array
    return jnp.clip(array, min=-limit, max=limit).astype(kind)


def setup_inputs(seed: int = 0) -> dict:
    splits = jax.random.split(jax.random.key(seed), 13)
    return {
        "disp": centred(splits[0], (3, NR, NLT, NCT), 0.3, 1.2, ((2, 4), (3, 8)), jnp.float32),
        "veloc": centred(splits[1], (3, NR, NLT, NCT), 1.0, 6.0, ((2, 4), (3, 8)), jnp.float32),
        "stiff": jnp.clip(jnp.exp(math.log(2.0) - 1.3862944 * jax.random.uniform(splits[2], (3, NR, NLT, NCT), jnp.float32) ** level_of(splits[2], (3, NR, NLT, NCT), ((2, 4), (3, 8)), -0.2, 0.2)), 0.5, 2.0),
        "mass": jnp.clip(jnp.exp(math.log(4.0) - 1.3862944 * jax.random.uniform(splits[3], (NR, NLT, NCT), jnp.float32) ** level_of(splits[3], (NR, NLT, NCT), ((1, 4), (2, 8)), -0.2, 0.2)), 1.0, 4.0),
        "road_height": centred(splits[4], (FACETS,), 0.3, 1.2, ((0, 4),), jnp.float32),
        "road_slope_x": jnp.clip(jax.random.uniform(splits[5], (FACETS,), jnp.float32, -0.3, 0.3) * level_of(splits[5], (FACETS,), ((0, 4),), -0.4, 0.0), -0.3, 0.3),
        "road_slope_y": jnp.clip(jax.random.uniform(splits[6], (FACETS,), jnp.float32, -0.3, 0.3) * level_of(splits[6], (FACETS,), ((0, 4),), -0.4, 0.0), -0.3, 0.3),
        "road_stiff": jnp.clip(jnp.exp(math.log(4.0) - 1.3862944 * jax.random.uniform(splits[7], (FACETS,), jnp.float32) ** level_of(splits[7], (FACETS,), ((0, 4),), -0.2, 0.2)), 1.0, 4.0),
        "tile_list": draw_tile_list(jax.random.fold_in(splits[12], 71), 0),
        "pair_node": draw_pair_node(jax.random.fold_in(splits[12], 71), 0),
        "pair_slot": draw_pair_slot(jax.random.fold_in(splits[12], 71), 0),
        "pair_count": draw_pair_count(jax.random.fold_in(splits[12], 71), 0),
    }


hardening = 0.5
time_step = 0.25


def stress_term(strain):
    squared = jnp.sum(strain * strain, axis=0, keepdims=True)
    return strain * (1.0 + hardening * squared)


def edge_force(padded, stiff_padded, which_dim):
    length = padded.shape[which_dim]
    strain = lax.slice_in_dim(padded, 1, length, axis=which_dim) - lax.slice_in_dim(padded, 0, length - 1, axis=which_dim)
    weights = lax.slice_in_dim(stiff_padded, 1, length, axis=which_dim - 1)
    tension = weights[None] * stress_term(strain)
    return lax.slice_in_dim(tension, 1, length - 1, axis=which_dim) - lax.slice_in_dim(tension, 0, length - 2, axis=which_dim)


def internal_force(displace, stiffness):
    radial = jnp.pad(displace, ((0, 0), (1, 1), (0, 0), (0, 0)))
    radial_stiff = jnp.pad(stiffness[0], ((1, 1), (0, 0), (0, 0)))
    summed = edge_force(radial, radial_stiff, 1)
    lateral = jnp.pad(displace, ((0, 0), (0, 0), (1, 1), (0, 0)))
    lateral_stiff = jnp.pad(stiffness[1], ((0, 0), (1, 1), (0, 0)))
    summed = summed + edge_force(lateral, lateral_stiff, 2)
    beside_all = jnp.concatenate([displace[..., -1:], displace, displace[..., :1]], axis=3)
    around_stiff = jnp.concatenate([stiffness[2][..., -1:], stiffness[2], stiffness[2][..., :1]], axis=2)
    return summed + edge_force(beside_all, around_stiff, 3)


def press(values):
    return values[6] * jnp.maximum(values[3] + values[4] * values[0] + values[5] * values[1] - values[2], 0.0)


def reference(disp, veloc, stiff, mass, road_height, road_slope_x, road_slope_y, road_stiff, tile_list, pair_node, pair_slot, pair_count):
    lateral_total = NL * BANDS
    around_total = NC * SECTORS
    sector = jnp.arange(SECTORS, dtype=jnp.int32)[:, None, None]
    band_index = jnp.arange(BANDS, dtype=jnp.int32)[None, :, None]
    where_node = ((band_index * NL + pair_node // NC) * around_total + sector * NC + pair_node % NC).reshape(-1)
    tile_pick = jnp.take_along_axis(tile_list, (pair_slot // TILE).astype(jnp.int32), axis=2)
    facet_id = (tile_pick * TILE + pair_slot % TILE).reshape(-1)
    slot_index = jnp.arange(PAIRS, dtype=jnp.int32)[None, None, :]
    live_slots = (slot_index < pair_count[:, :, None]).reshape(-1)
    facet_values = jnp.stack([road_height[facet_id], road_slope_x[facet_id], road_slope_y[facet_id], road_stiff[facet_id]])
    displace = disp
    velocity = veloc
    facet_load = jnp.zeros((FACETS,), jnp.float32)
    for step_index in range(STEPS):
        outer_layer = displace[:, NR - 1].reshape(3, -1)
        picked = outer_layer[:, where_node]
        values = jnp.concatenate([picked, facet_values], axis=0)
        normal_force = jnp.where(live_slots, press(values), 0.0)
        contact = jnp.stack([-values[4] * normal_force, -values[5] * normal_force, normal_force])
        outer_force = jnp.zeros_like(outer_layer).at[:, where_node].add(contact)
        forces = internal_force(displace, stiff)
        forces = forces.at[:, NR - 1].add(outer_force.reshape(3, lateral_total, around_total))
        velocity = velocity + time_step * forces / mass[None]
        displace = displace + time_step * velocity
        facet_load = facet_load + jnp.zeros((FACETS,), jnp.float32).at[facet_id].add(normal_force)
    return velocity, facet_load
```

```python
import functools

import jax
import jax.numpy as jnp
from jax import lax
from jax.experimental import pallas as pl
from jax.experimental.pallas import tpu as pltpu
from jax.sharding import PartitionSpec as P

TILE = 256
LANES = 128
GROUP = 1024

hardening = 0.5
time_step = 0.25

MESH = pl.DeviceIdType.MESH
NT = (((1,), (1,)), ((), ()))


def split_two(x):
    high = x.astype(jnp.bfloat16).astype(jnp.float32)
    return high, x - high


def tension(weights, strain):
    squared = strain[0] * strain[0] + strain[1] * strain[1] + strain[2] * strain[2]
    scaled = weights * (1.0 + hardening * squared)
    return [scaled * s for s in strain]


def kernel(
    n_blk,
    n_road,
    lat,
    in_kernel_sum,
    disp,
    veloc,
    stiff,
    mass,
    height,
    slope_x,
    slope_y,
    road_stiff,
    tiles,
    nodes,
    slots,
    count,
    v_out,
    load_out,
    u1,
    v1,
    force,
    node_hot,
    facet_hot,
    facet_vals,
    facet_all,
    table,
    up_send,
    down_send,
    up_recv,
    down_recv,
    side_up_send,
    side_down_send,
    side_up_recv,
    side_down_recv,
    halo_sems,
    facet_sems,
    *reduction,
):
    b = lax.axis_index("blk")
    r = lax.axis_index("road")
    rows = disp.shape[1]
    layers = rows // lat
    groups = nodes.shape[1] // GROUP
    n_rows = table.shape[1]
    half = table.shape[1] // tiles.shape[1]
    patch_rows = height.shape[0]

    def road_peer(offset):
        return {"blk": b, "road": lax.rem(r + offset, n_road)}

    def blk_peer(offset):
        return {"blk": lax.rem(b + offset, n_blk), "road": r}

    blk_offsets = range(1, n_blk) if in_kernel_sum else sorted({1, n_blk - 1})
    barrier = pltpu.get_barrier_semaphore()
    for offset in blk_offsets:
        pl.semaphore_signal(barrier, inc=1, device_id=blk_peer(offset), device_id_type=MESH)
    for offset in range(1, n_road):
        pl.semaphore_signal(barrier, inc=1, device_id=road_peer(offset), device_id_type=MESH)

    def fill_faces(step, source):
        for c in range(3):
            turned = source[c].T
            up_send[step, c : c + 1, :] = turned[LANES - 1 : LANES, :]
            down_send[step, c : c + 1, :] = turned[0:1, :]
            side_up_send[step, c] = source[c, pl.ds(lat - 1, layers, stride=lat), :]
            side_down_send[step, c] = source[c, pl.ds(0, layers, stride=lat), :]
        if step == 0:
            down_send[step, 3:4, :] = stiff[2].T[0:1, :]
            side_down_send[step, 3] = stiff[1, pl.ds(0, layers, stride=lat), :]

    def halo_copies(step):
        plan = (
            (up_send, up_recv, blk_peer(1)),
            (down_send, down_recv, blk_peer(n_blk - 1)),
            (side_up_send, side_up_recv, road_peer(1)),
            (side_down_send, side_down_recv, road_peer(n_road - 1)),
        )
        return [
            pltpu.make_async_remote_copy(
                src_ref=src.at[step],
                dst_ref=dst.at[step],
                send_sem=halo_sems.at[step, 0, i],
                recv_sem=halo_sems.at[step, 1, i],
                device_id=peer,
                device_id_type=MESH,
            )
            for i, (src, dst, peer) in enumerate(plan)
        ]

    fill_faces(0, disp)

    def make_hot(g, _):
        at = pl.ds(pl.multiple_of(g * GROUP, GROUP), GROUP)
        lane = lax.broadcasted_iota(jnp.int32, (LANES, GROUP), 0)
        node_lane = nodes[:, at] & (LANES - 1)
        slot_lane = slots[:, at] & (LANES - 1)
        node_hot[g] = jnp.where(lane == node_lane, 1.0, 0.0).astype(jnp.bfloat16)
        facet_hot[g] = jnp.where(lane == slot_lane, 1.0, 0.0).astype(jnp.bfloat16)
        return 0

    lax.fori_loop(0, groups, make_hot, 0)

    pl.semaphore_wait(barrier, len(blk_offsets) + n_road - 1)
    halos0 = halo_copies(0)
    for copy in halos0:
        copy.start()
    own = (height, slope_x, slope_y, road_stiff)
    facet_copies = []
    for offset in range(1, n_road):
        for a in range(4):
            copy = pltpu.make_async_remote_copy(
                src_ref=own[a],
                dst_ref=facet_all.at[a * n_road + r],
                send_sem=facet_sems.at[0, a, offset - 1],
                recv_sem=facet_sems.at[1, a, offset - 1],
                device_id=road_peer(offset),
                device_id_type=MESH,
            )
            copy.start()
            facet_copies.append(copy)
    for a in range(4):
        facet_all[a * n_road + r] = own[a][...]

    lat_index = lax.broadcasted_iota(jnp.int32, (lat, LANES), 0)
    lane_index = lax.broadcasted_iota(jnp.int32, (lat, LANES), 1)

    def layer_rows(k):
        return pl.ds(pl.multiple_of(k * lat, lat), lat)

    def inside(source, k, above, rim):
        at = layer_rows(k)
        u = [source[c, at, :] for c in range(3)]
        if rim:
            strain = u
        else:
            below = layer_rows(k - 1)
            strain = [u[c] - source[c, below, :] for c in range(3)]
        radial = tension(stiff[0, at, :], strain)
        side = tension(stiff[1, at, :], [x - pltpu.roll(x, 1, 0) for x in u])
        around = tension(stiff[2, at, :], [x - pltpu.roll(x, 1, 1) for x in u])
        for c in range(3):
            t = jnp.where(lat_index == 0, 0.0, side[c])
            w = jnp.where(lane_index == 0, 0.0, around[c])
            force[c, at, :] = (
                (above[c] - radial[c])
                + (pltpu.roll(t, lat - 1, 0) - t)
                + (pltpu.roll(w, LANES - 1, 1) - w)
            )
        return radial

    def interior(source):
        nothing = tuple(jnp.zeros((lat, LANES), jnp.float32) for _ in range(3))

        def body(i, above):
            return tuple(inside(source, layers - 1 - i, above, False))

        above = lax.fori_loop(0, layers - 1, body, nothing)
        inside(source, 0, above, True)

    def rim_force(step):
        stiff_around = down_recv[0, 3:4, :]
        own_around = down_send[0, 3:4, :]
        low = tension(own_around, [down_send[step, c : c + 1, :] - up_recv[step, c : c + 1, :] for c in range(3)])
        high = tension(stiff_around, [down_recv[step, c : c + 1, :] - up_send[step, c : c + 1, :] for c in range(3)])
        place = lax.broadcasted_iota(jnp.int32, (LANES, rows), 0)
        for c in range(3):
            turned = jnp.where(place == 0, -low[c], jnp.where(place == LANES - 1, high[c], 0.0))
            force[c] = force[c] + turned.T
        first = jnp.where(r == 0, 0.0, 1.0)
        last = jnp.where(r == n_road - 1, 0.0, 1.0)
        low = tension(
            side_down_send[0, 3], [side_down_send[step, c] - first * side_up_recv[step, c] for c in range(3)]
        )
        high = tension(
            last * side_down_recv[0, 3], [side_down_recv[step, c] - side_up_send[step, c] for c in range(3)]
        )
        for c in range(3):
            at = pl.ds(0, layers, stride=lat)
            force[c, at, :] = force[c, at, :] - low[c]
            at = pl.ds(lat - 1, layers, stride=lat)
            force[c, at, :] = force[c, at, :] + high[c]

    live_count = count[0, 0]

    def contact(source):
        outer = [source[c, rows - lat : rows, :] for c in range(3)]
        parts = [split_two(x) for x in outer]
        picked_from = jnp.concatenate([p[0] for p in parts] + [p[1] for p in parts], axis=0).astype(jnp.bfloat16)
        node_row = lax.broadcasted_iota(jnp.int32, (lat, GROUP), 0)
        facet_row = lax.broadcasted_iota(jnp.int32, (n_rows, GROUP), 0)
        slot_lane = lax.broadcasted_iota(jnp.int32, (1, GROUP), 1)

        def body(g, carry):
            pushed, loads = carry
            at = pl.ds(pl.multiple_of(g * GROUP, GROUP), GROUP)
            on_node = node_row == (nodes[:, at] >> 7)
            on_facet = facet_row == (slots[:, at] >> 7)
            found = jnp.dot(picked_from, node_hot[g], preferred_element_type=jnp.float32)
            u = []
            for c in range(3):
                both = found[c * lat : (c + 1) * lat] + found[(3 + c) * lat : (4 + c) * lat]
                u.append(jnp.sum(jnp.where(on_node, both, 0.0), axis=0, keepdims=True))
            values = facet_vals[g]
            h, sx, sy, ks = (values[a : a + 1, :] for a in range(4))
            live = slot_lane + g * GROUP < live_count
            normal = jnp.where(live, ks * jnp.maximum(h + sx * u[0] + sy * u[1] - u[2], 0.0), 0.0)
            high, low = zip(*[split_two(x) for x in (-sx * normal, -sy * normal, normal)])
            spread = jnp.concatenate([jnp.where(on_node, x, 0.0) for x in high + low], axis=0)
            pushed = pushed + lax.dot_general(
                spread.astype(jnp.bfloat16), node_hot[g], NT, preferred_element_type=jnp.float32
            )
            heaped = jnp.concatenate([jnp.where(on_facet, x, 0.0) for x in (high[2], low[2])], axis=0)
            loads = loads + lax.dot_general(
                heaped.astype(jnp.bfloat16), facet_hot[g], NT, preferred_element_type=jnp.float32
            )
            return pushed, loads

        pushed, loads = lax.fori_loop(
            0,
            groups,
            body,
            (jnp.zeros((6 * lat, LANES), jnp.float32), jnp.zeros((2 * n_rows, LANES), jnp.float32)),
        )
        outer_force = [pushed[c * lat : (c + 1) * lat] + pushed[(3 + c) * lat : (4 + c) * lat] for c in range(3)]
        return outer_force, loads[:n_rows] + loads[n_rows:]

    def add_outer(outer_force):
        for c in range(3):
            force[c, rows - lat : rows, :] = force[c, rows - lat : rows, :] + outer_force[c]

    interior(disp)

    for copy in facet_copies:
        copy.wait()
    for j in range(tiles.shape[1]):
        for i in range(half):
            row = tiles[0, j] * half + i
            for a in range(4):
                table[a, j * half + i : j * half + i + 1, :] = facet_all[
                    a * n_road + row // patch_rows, pl.ds(row % patch_rows, 1), :
                ]
    parts = [split_two(table[a]) for a in range(4)]
    looked_from = jnp.concatenate([p[0] for p in parts] + [p[1] for p in parts], axis=0).astype(jnp.bfloat16)

    def look_up(g, _):
        at = pl.ds(pl.multiple_of(g * GROUP, GROUP), GROUP)
        on_facet = lax.broadcasted_iota(jnp.int32, (n_rows, GROUP), 0) == (slots[:, at] >> 7)
        found = jnp.dot(looked_from, facet_hot[g], preferred_element_type=jnp.float32)
        for a in range(4):
            both = found[a * n_rows : (a + 1) * n_rows] + found[(4 + a) * n_rows : (5 + a) * n_rows]
            facet_vals[g, a : a + 1, :] = jnp.sum(jnp.where(on_facet, both, 0.0), axis=0, keepdims=True)
        return 0

    lax.fori_loop(0, groups, look_up, 0)
    outer_force, loads0 = contact(disp)
    add_outer(outer_force)

    for copy in halos0:
        copy.wait()
    rim_force(0)

    def advance(k, _):
        at = layer_rows(k)
        scale = time_step / mass[at, :]
        for c in range(3):
            v = veloc[c, at, :] + scale * force[c, at, :]
            v1[c, at, :] = v
            u1[c, at, :] = disp[c, at, :] + time_step * v
        return 0

    lax.fori_loop(0, layers, advance, 0)
    fill_faces(1, u1)
    halos1 = halo_copies(1)
    for copy in halos1:
        copy.start()

    outer_force, loads1 = contact(u1)
    loads = loads0 + loads1

    def dense(shape, row_of):
        row = row_of(shape)
        total = jnp.zeros(shape, jnp.float32)
        for j in range(n_rows):
            here = tiles[0, j // half] * half + j % half
            line = loads[j : j + 1, :].reshape((1,) * (len(shape) - 1) + (LANES,))
            total = total + jnp.where(row == here, line, 0.0)
        return total

    if in_kernel_sum:
        spread_out, road_recv, reduced, blk_recv, road_sems, blk_sems = reduction
        chunk_rows = load_out.shape[0]
        for to in range(n_road):
            spread_out[to] = dense(
                (n_blk, chunk_rows, LANES),
                lambda s: (lax.broadcasted_iota(jnp.int32, s, 0) * n_road + to) * chunk_rows
                + lax.broadcasted_iota(jnp.int32, s, 1),
            )
        road_copies = []
        for offset in range(1, n_road):
            copy = pltpu.make_async_remote_copy(
                src_ref=spread_out.at[lax.rem(r + offset, n_road)],
                dst_ref=road_recv.at[offset - 1],
                send_sem=road_sems.at[0, offset - 1],
                recv_sem=road_sems.at[1, offset - 1],
                device_id=road_peer(offset),
                device_id_type=MESH,
            )
            copy.start()
            road_copies.append(copy)
    else:
        load_out[...] = dense(load_out.shape, lambda s: lax.broadcasted_iota(jnp.int32, s, 0))

    interior(u1)
    add_outer(outer_force)

    if in_kernel_sum:
        for copy in road_copies:
            copy.wait()
        total = spread_out[r]
        for i in range(n_road - 1):
            total = total + road_recv[i]
        reduced[...] = total
        blk_copies = []
        for offset in range(1, n_blk):
            copy = pltpu.make_async_remote_copy(
                src_ref=reduced.at[lax.rem(b + offset, n_blk)],
                dst_ref=blk_recv.at[offset - 1],
                send_sem=blk_sems.at[0, offset - 1],
                recv_sem=blk_sems.at[1, offset - 1],
                device_id=blk_peer(offset),
                device_id_type=MESH,
            )
            copy.start()
            blk_copies.append(copy)

    for copy in halos1:
        copy.wait()
    rim_force(1)

    def finish(k, _):
        at = layer_rows(k)
        scale = time_step / mass[at, :]
        for c in range(3):
            v_out[c, at, :] = v1[c, at, :] + scale * force[c, at, :]
        return 0

    lax.fori_loop(0, layers, finish, 0)

    if in_kernel_sum:
        for copy in blk_copies:
            copy.wait()
        total = reduced[b]
        for i in range(n_blk - 1):
            total = total + blk_recv[i]
        load_out[...] = total


def on_device(
    n_blk,
    n_road,
    disp,
    veloc,
    stiff,
    mass,
    road_height,
    road_slope_x,
    road_slope_y,
    road_stiff,
    tile_list,
    pair_node,
    pair_slot,
    pair_count,
):
    _, layers, lat, lanes = disp.shape
    rows = layers * lat
    pairs = pair_node.shape[-1]
    groups = pairs // GROUP
    tiles_need = tile_list.shape[-1]
    patch_rows = road_height.shape[0] // LANES
    total_rows = patch_rows * n_road
    table_rows = tiles_need * TILE // LANES
    devices = n_blk * n_road
    in_kernel_sum = total_rows % devices == 0
    f32 = jnp.float32
    if in_kernel_sum:
        load_shape = (total_rows // devices, LANES)
    else:
        load_shape = (total_rows, LANES)
    scratch = [
        pltpu.VMEM((3, rows, lanes), f32),
        pltpu.VMEM((3, rows, lanes), f32),
        pltpu.VMEM((3, rows, lanes), f32),
        pltpu.VMEM((groups, LANES, GROUP), jnp.bfloat16),
        pltpu.VMEM((groups, LANES, GROUP), jnp.bfloat16),
        pltpu.VMEM((groups, 4, GROUP), f32),
        pltpu.VMEM((4 * n_road, patch_rows, LANES), f32),
        pltpu.VMEM((4, table_rows, LANES), f32),
        pltpu.VMEM((2, 3, rows), f32),
        pltpu.VMEM((2, 4, rows), f32),
        pltpu.VMEM((2, 3, rows), f32),
        pltpu.VMEM((2, 4, rows), f32),
        pltpu.VMEM((2, 3, layers, lanes), f32),
        pltpu.VMEM((2, 4, layers, lanes), f32),
        pltpu.VMEM((2, 3, layers, lanes), f32),
        pltpu.VMEM((2, 4, layers, lanes), f32),
        pltpu.SemaphoreType.DMA((2, 2, 4)),
        pltpu.SemaphoreType.DMA((2, 4, n_road - 1)),
    ]
    if in_kernel_sum:
        scratch += [
            pltpu.VMEM((n_road, n_blk) + load_shape, f32),
            pltpu.VMEM((n_road - 1, n_blk) + load_shape, f32),
            pltpu.VMEM((n_blk,) + load_shape, f32),
            pltpu.VMEM((n_blk - 1,) + load_shape, f32),
            pltpu.SemaphoreType.DMA((2, n_road - 1)),
            pltpu.SemaphoreType.DMA((2, n_blk - 1)),
        ]
    vmem = pl.BlockSpec(memory_space=pltpu.VMEM)
    smem = pl.BlockSpec(memory_space=pltpu.SMEM)
    velocity, load = pl.pallas_call(
        functools.partial(kernel, n_blk, n_road, lat, in_kernel_sum),
        out_shape=(
            jax.ShapeDtypeStruct((3, rows, lanes), f32),
            jax.ShapeDtypeStruct(load_shape, f32),
        ),
        in_specs=[vmem] * 8 + [smem, vmem, vmem, smem],
        out_specs=(vmem, vmem),
        scratch_shapes=scratch,
        compiler_params=pltpu.CompilerParams(collective_id=0, has_side_effects=True),
    )(
        disp.reshape(3, rows, lanes),
        veloc.reshape(3, rows, lanes),
        stiff.reshape(3, rows, lanes),
        mass.reshape(rows, lanes),
        road_height.reshape(patch_rows, LANES),
        road_slope_x.reshape(patch_rows, LANES),
        road_slope_y.reshape(patch_rows, LANES),
        road_stiff.reshape(patch_rows, LANES),
        tile_list.reshape(1, tiles_need),
        pair_node.reshape(1, pairs),
        pair_slot.reshape(1, pairs),
        pair_count.reshape(1, 1),
    )
    load = load.reshape(-1)
    if not in_kernel_sum:
        load = lax.psum_scatter(load, ("blk", "road"), scatter_dimension=0, tiled=True)
    return velocity.reshape(disp.shape), load


def solution(mesh):
    in_specs = (
        P(None, None, "road", "blk"),
        P(None, None, "road", "blk"),
        P(None, None, "road", "blk"),
        P(None, "road", "blk"),
        P("road"),
        P("road"),
        P("road"),
        P("road"),
        P("blk", "road", None),
        P("blk", "road", None),
        P("blk", "road", None),
        P("blk", "road"),
    )
    out_specs = (P(None, None, "road", "blk"), P(("blk", "road")))
    body = functools.partial(on_device, mesh.shape["blk"], mesh.shape["road"])
    return jax.shard_map(body, mesh=mesh, in_specs=in_specs, out_specs=out_specs, check_vma=False)
```

```python
import functools

import jax
import jax.numpy as jnp
from jax import lax
from jax.experimental import pallas as pl
from jax.experimental.pallas import tpu as pltpu
from jax.sharding import PartitionSpec as P

TILE = 256
LANES = 128
GROUP = 1024

hardening = 0.5
time_step = 0.25

MESH = pl.DeviceIdType.MESH
NT = (((1,), (1,)), ((), ()))


def split_two(x):
    high = x.astype(jnp.bfloat16).astype(jnp.float32)
    return high, x - high


def tension(weights, strain):
    squared = strain[0] * strain[0] + strain[1] * strain[1] + strain[2] * strain[2]
    scaled = weights * (1.0 + hardening * squared)
    return [scaled * s for s in strain]


def kernel(
    n_blk,
    n_road,
    lat,
    in_kernel_sum,
    disp_in,
    veloc_in,
    stiff_in,
    mass_in,
    height,
    slope_x,
    slope_y,
    road_stiff,
    tiles,
    nodes_in,
    slots_in,
    count,
    v_out,
    load_out,
    disp,
    veloc,
    stiff,
    mass,
    nodes,
    slots,
    in_sems,
    own_sems,
    picked_vals,
    u1,
    v1,
    force,
    node_hot,
    facet_hot,
    facet_vals,
    facet_all,
    table,
    up_send,
    down_send,
    up_recv,
    down_recv,
    side_up_send,
    side_down_send,
    side_up_recv,
    side_down_recv,
    halo_sems,
    facet_sems,
    *reduction,
):
    b = lax.axis_index("blk")
    r = lax.axis_index("road")
    rows = disp.shape[1]
    layers = rows // lat
    groups = nodes.shape[1] // GROUP
    n_rows = table.shape[1]
    half = table.shape[1] // tiles.shape[1]
    patch_rows = height.shape[0]

    def road_peer(offset):
        return {"blk": b, "road": lax.rem(r + offset, n_road)}

    def blk_peer(offset):
        return {"blk": lax.rem(b + offset, n_blk), "road": r}

    blk_offsets = range(1, n_blk) if in_kernel_sum else sorted({1, n_blk - 1})
    barrier = pltpu.get_barrier_semaphore()
    for offset in blk_offsets:
        pl.semaphore_signal(barrier, inc=1, device_id=blk_peer(offset), device_id_type=MESH)
    for offset in range(1, n_road):
        pl.semaphore_signal(barrier, inc=1, device_id=road_peer(offset), device_id_type=MESH)

    def fill_faces(step, source):
        for c in range(3):
            turned = source[c].T
            up_send[step, c : c + 1, :] = turned[LANES - 1 : LANES, :]
            down_send[step, c : c + 1, :] = turned[0:1, :]
            side_up_send[step, c] = source[c, pl.ds(lat - 1, layers, stride=lat), :]
            side_down_send[step, c] = source[c, pl.ds(0, layers, stride=lat), :]
        if step == 0:
            down_send[step, 3:4, :] = stiff[2].T[0:1, :]
            side_down_send[step, 3] = stiff[1, pl.ds(0, layers, stride=lat), :]

    def halo_copies(step):
        plan = (
            (up_send, up_recv, blk_peer(1)),
            (down_send, down_recv, blk_peer(n_blk - 1)),
            (side_up_send, side_up_recv, road_peer(1)),
            (side_down_send, side_down_recv, road_peer(n_road - 1)),
        )
        return [
            pltpu.make_async_remote_copy(
                src_ref=src.at[step],
                dst_ref=dst.at[step],
                send_sem=halo_sems.at[step, 0, i],
                recv_sem=halo_sems.at[step, 1, i],
                device_id=peer,
                device_id_type=MESH,
            )
            for i, (src, dst, peer) in enumerate(plan)
        ]

    loads_in = [
        pltpu.make_async_copy(src, dst, in_sems.at[i])
        for i, (src, dst) in enumerate(
            (
                (disp_in, disp),
                (stiff_in, stiff),
                (nodes_in, nodes),
                (slots_in, slots),
                (mass_in, mass),
                (veloc_in, veloc),
            )
        )
    ]
    for copy in loads_in:
        copy.start()
    own = (height, slope_x, slope_y, road_stiff)
    own_copies = [
        pltpu.make_async_copy(own[a], facet_all.at[a * n_road + r], own_sems.at[a]) for a in range(4)
    ]
    for copy in own_copies:
        copy.start()
    for copy in loads_in[:2]:
        copy.wait()
    fill_faces(0, disp)
    for copy in loads_in[2:4]:
        copy.wait()

    def make_hot(g, _):
        at = pl.ds(pl.multiple_of(g * GROUP, GROUP), GROUP)
        lane = lax.broadcasted_iota(jnp.int32, (LANES, GROUP), 0)
        node_lane = nodes[:, at] & (LANES - 1)
        slot_lane = slots[:, at] & (LANES - 1)
        node_hot[g] = jnp.where(lane == node_lane, 1.0, 0.0).astype(jnp.bfloat16)
        facet_hot[g] = jnp.where(lane == slot_lane, 1.0, 0.0).astype(jnp.bfloat16)
        return 0

    lax.fori_loop(0, groups, make_hot, 0, unroll=2)

    pl.semaphore_wait(barrier, len(blk_offsets) + n_road - 1)
    halos0 = halo_copies(0)
    for copy in halos0:
        copy.start()
    facet_copies = []
    for offset in range(1, n_road):
        for a in range(4):
            copy = pltpu.make_async_remote_copy(
                src_ref=own[a],
                dst_ref=facet_all.at[a * n_road + r],
                send_sem=facet_sems.at[0, a, offset - 1],
                recv_sem=facet_sems.at[1, a, offset - 1],
                device_id=road_peer(offset),
                device_id_type=MESH,
            )
            copy.start()
            facet_copies.append(copy)
    lat_index = lax.broadcasted_iota(jnp.int32, (lat, LANES), 0)
    lane_index = lax.broadcasted_iota(jnp.int32, (lat, LANES), 1)

    def layer_rows(k):
        return pl.ds(pl.multiple_of(k * lat, lat), lat)

    def inside(source, k, above, rim):
        at = layer_rows(k)
        u = [source[c, at, :] for c in range(3)]
        if rim:
            strain = u
        else:
            below = layer_rows(k - 1)
            strain = [u[c] - source[c, below, :] for c in range(3)]
        radial = tension(stiff[0, at, :], strain)
        side = tension(stiff[1, at, :], [x - pltpu.roll(x, 1, 0) for x in u])
        around = tension(stiff[2, at, :], [x - pltpu.roll(x, 1, 1) for x in u])
        for c in range(3):
            t = jnp.where(lat_index == 0, 0.0, side[c])
            w = jnp.where(lane_index == 0, 0.0, around[c])
            force[c, at, :] = (
                (above[c] - radial[c])
                + (pltpu.roll(t, lat - 1, 0) - t)
                + (pltpu.roll(w, LANES - 1, 1) - w)
            )
        return radial

    def interior(source):
        nothing = tuple(jnp.zeros((lat, LANES), jnp.float32) for _ in range(3))

        def body(i, above):
            return tuple(inside(source, layers - 1 - i, above, False))

        above = lax.fori_loop(0, layers - 1, body, nothing, unroll=3)
        inside(source, 0, above, True)

    def rim_force(step):
        stiff_around = down_recv[0, 3:4, :]
        own_around = down_send[0, 3:4, :]
        low = tension(own_around, [down_send[step, c : c + 1, :] - up_recv[step, c : c + 1, :] for c in range(3)])
        high = tension(stiff_around, [down_recv[step, c : c + 1, :] - up_send[step, c : c + 1, :] for c in range(3)])
        place = lax.broadcasted_iota(jnp.int32, (LANES, rows), 0)
        for c in range(3):
            turned = jnp.where(place == 0, -low[c], jnp.where(place == LANES - 1, high[c], 0.0))
            force[c] = force[c] + turned.T
        first = jnp.where(r == 0, 0.0, 1.0)
        last = jnp.where(r == n_road - 1, 0.0, 1.0)
        low = tension(
            side_down_send[0, 3], [side_down_send[step, c] - first * side_up_recv[step, c] for c in range(3)]
        )
        high = tension(
            last * side_down_recv[0, 3], [side_down_recv[step, c] - side_up_send[step, c] for c in range(3)]
        )
        for c in range(3):
            at = pl.ds(0, layers, stride=lat)
            force[c, at, :] = force[c, at, :] - low[c]
            at = pl.ds(lat - 1, layers, stride=lat)
            force[c, at, :] = force[c, at, :] + high[c]

    live_count = count[0, 0]

    node_row = lax.broadcasted_iota(jnp.int32, (lat, GROUP), 0)
    facet_row = lax.broadcasted_iota(jnp.int32, (n_rows, GROUP), 0)
    slot_lane = lax.broadcasted_iota(jnp.int32, (1, GROUP), 1)

    def split_rows(arrays):
        parts = [split_two(x) for x in arrays]
        return jnp.concatenate([p[0] for p in parts] + [p[1] for p in parts], axis=0).astype(jnp.bfloat16)

    def group_at(g):
        return pl.ds(pl.multiple_of(g * GROUP, GROUP), GROUP)

    def look(table_rows, hot, mask, height_of):
        found = jnp.dot(table_rows, hot, preferred_element_type=jnp.float32)
        arrays = found.shape[0] // (2 * height_of)
        out = []
        for a in range(arrays):
            both = (
                found[a * height_of : (a + 1) * height_of]
                + found[(arrays + a) * height_of : (arrays + a + 1) * height_of]
            )
            out.append(jnp.sum(jnp.where(mask, both, 0.0), axis=0, keepdims=True))
        return out

    def outer_rows(source):
        return split_rows([source[c, rows - lat : rows, :] for c in range(3)])

    def on_nodes(g):
        return node_row == (nodes[:, group_at(g)] >> 7)

    def contact(find_nodes, find_facets):
        def body(g, carry):
            pushed, loads = carry
            on_node = on_nodes(g)
            on_facet = facet_row == (slots[:, group_at(g)] >> 7)
            u = find_nodes(g, on_node)
            h, sx, sy, ks = find_facets(g, on_facet)
            live = slot_lane + g * GROUP < live_count
            normal = jnp.where(live, ks * jnp.maximum(h + sx * u[0] + sy * u[1] - u[2], 0.0), 0.0)
            high, low = zip(*[split_two(x) for x in (-sx * normal, -sy * normal, normal)])
            spread = jnp.concatenate([jnp.where(on_node, x, 0.0) for x in high + low], axis=0)
            pushed = pushed + lax.dot_general(
                spread.astype(jnp.bfloat16), node_hot[g], NT, preferred_element_type=jnp.float32
            )
            heaped = jnp.concatenate([jnp.where(on_facet, x, 0.0) for x in (high[2], low[2])], axis=0)
            loads = loads + lax.dot_general(
                heaped.astype(jnp.bfloat16), facet_hot[g], NT, preferred_element_type=jnp.float32
            )
            return pushed, loads

        pushed, loads = lax.fori_loop(
            0,
            groups,
            body,
            (jnp.zeros((6 * lat, LANES), jnp.float32), jnp.zeros((2 * n_rows, LANES), jnp.float32)),
            unroll=4,
        )
        outer_force = [pushed[c * lat : (c + 1) * lat] + pushed[(3 + c) * lat : (4 + c) * lat] for c in range(3)]
        return outer_force, loads[:n_rows] + loads[n_rows:]

    def add_outer(outer_force):
        for c in range(3):
            force[c, rows - lat : rows, :] = force[c, rows - lat : rows, :] + outer_force[c]

    interior(disp)
    first_outer = outer_rows(disp)

    def pick_first(g, _):
        for c, x in enumerate(look(first_outer, node_hot[g], on_nodes(g), lat)):
            picked_vals[g, c : c + 1, :] = x
        return 0

    lax.fori_loop(0, groups, pick_first, 0, unroll=4)

    for copy in own_copies + loads_in[4:]:
        copy.wait()
    for copy in facet_copies:
        copy.wait()
    for j in range(tiles.shape[1]):
        for i in range(half):
            row = tiles[0, j] * half + i
            for a in range(4):
                table[a, j * half + i : j * half + i + 1, :] = facet_all[
                    a * n_road + row // patch_rows, pl.ds(row % patch_rows, 1), :
                ]
    looked_from = split_rows([table[a] for a in range(4)])

    def first_nodes(g, on_node):
        return [picked_vals[g, c : c + 1, :] for c in range(3)]

    def first_facets(g, on_facet):
        values = look(looked_from, facet_hot[g], on_facet, n_rows)
        for a in range(4):
            facet_vals[g, a : a + 1, :] = values[a]
        return values

    outer_force, loads0 = contact(first_nodes, first_facets)
    add_outer(outer_force)

    for copy in halos0:
        copy.wait()
    rim_force(0)

    def advance(k, _):
        at = layer_rows(k)
        scale = time_step / mass[at, :]
        for c in range(3):
            v = veloc[c, at, :] + scale * force[c, at, :]
            v1[c, at, :] = v
            u1[c, at, :] = disp[c, at, :] + time_step * v
        return 0

    lax.fori_loop(0, layers, advance, 0)
    fill_faces(1, u1)
    halos1 = halo_copies(1)
    for copy in halos1:
        copy.start()

    second_outer = outer_rows(u1)
    outer_force, loads1 = contact(
        lambda g, on_node: look(second_outer, node_hot[g], on_node, lat),
        lambda g, on_facet: [facet_vals[g, a : a + 1, :] for a in range(4)],
    )
    loads = loads0 + loads1

    def dense(shape, row_of):
        row = row_of(shape)
        total = jnp.zeros(shape, jnp.float32)
        for j in range(n_rows):
            here = tiles[0, j // half] * half + j % half
            line = loads[j : j + 1, :].reshape((1,) * (len(shape) - 1) + (LANES,))
            total = total + jnp.where(row == here, line, 0.0)
        return total

    if in_kernel_sum:
        spread_out, road_recv, reduced, blk_recv, road_sems, blk_sems = reduction
        chunk_rows = load_out.shape[0]
        for to in range(n_road):
            spread_out[to] = dense(
                (n_blk, chunk_rows, LANES),
                lambda s: (lax.broadcasted_iota(jnp.int32, s, 0) * n_road + to) * chunk_rows
                + lax.broadcasted_iota(jnp.int32, s, 1),
            )
        road_copies = []
        for offset in range(1, n_road):
            copy = pltpu.make_async_remote_copy(
                src_ref=spread_out.at[lax.rem(r + offset, n_road)],
                dst_ref=road_recv.at[offset - 1],
                send_sem=road_sems.at[0, offset - 1],
                recv_sem=road_sems.at[1, offset - 1],
                device_id=road_peer(offset),
                device_id_type=MESH,
            )
            copy.start()
            road_copies.append(copy)
    else:
        load_out[...] = dense(load_out.shape, lambda s: lax.broadcasted_iota(jnp.int32, s, 0))

    interior(u1)
    add_outer(outer_force)

    if in_kernel_sum:
        for copy in road_copies:
            copy.wait()
        total = spread_out[r]
        for i in range(n_road - 1):
            total = total + road_recv[i]
        reduced[...] = total
        blk_copies = []
        for offset in range(1, n_blk):
            copy = pltpu.make_async_remote_copy(
                src_ref=reduced.at[lax.rem(b + offset, n_blk)],
                dst_ref=blk_recv.at[offset - 1],
                send_sem=blk_sems.at[0, offset - 1],
                recv_sem=blk_sems.at[1, offset - 1],
                device_id=blk_peer(offset),
                device_id_type=MESH,
            )
            copy.start()
            blk_copies.append(copy)

    for copy in halos1:
        copy.wait()
    rim_force(1)

    def finish(k, _):
        at = layer_rows(k)
        scale = time_step / mass[at, :]
        for c in range(3):
            v_out[c, at, :] = v1[c, at, :] + scale * force[c, at, :]
        return 0

    lax.fori_loop(0, layers, finish, 0)

    if in_kernel_sum:
        for copy in blk_copies:
            copy.wait()
        total = reduced[b]
        for i in range(n_blk - 1):
            total = total + blk_recv[i]
        load_out[...] = total


def on_device(
    n_blk,
    n_road,
    disp,
    veloc,
    stiff,
    mass,
    road_height,
    road_slope_x,
    road_slope_y,
    road_stiff,
    tile_list,
    pair_node,
    pair_slot,
    pair_count,
):
    _, layers, lat, lanes = disp.shape
    rows = layers * lat
    pairs = pair_node.shape[-1]
    groups = pairs // GROUP
    tiles_need = tile_list.shape[-1]
    patch_rows = road_height.shape[0] // LANES
    total_rows = patch_rows * n_road
    table_rows = tiles_need * TILE // LANES
    devices = n_blk * n_road
    in_kernel_sum = total_rows % devices == 0
    f32 = jnp.float32
    if in_kernel_sum:
        load_shape = (total_rows // devices, LANES)
    else:
        load_shape = (total_rows, LANES)
    scratch = [
        pltpu.VMEM((3, rows, lanes), f32),
        pltpu.VMEM((3, rows, lanes), f32),
        pltpu.VMEM((3, rows, lanes), f32),
        pltpu.VMEM((rows, lanes), f32),
        pltpu.VMEM((1, pairs), jnp.int32),
        pltpu.VMEM((1, pairs), jnp.int32),
        pltpu.SemaphoreType.DMA((6,)),
        pltpu.SemaphoreType.DMA((4,)),
        pltpu.VMEM((groups, 3, GROUP), f32),
        pltpu.VMEM((3, rows, lanes), f32),
        pltpu.VMEM((3, rows, lanes), f32),
        pltpu.VMEM((3, rows, lanes), f32),
        pltpu.VMEM((groups, LANES, GROUP), jnp.bfloat16),
        pltpu.VMEM((groups, LANES, GROUP), jnp.bfloat16),
        pltpu.VMEM((groups, 4, GROUP), f32),
        pltpu.VMEM((4 * n_road, patch_rows, LANES), f32),
        pltpu.VMEM((4, table_rows, LANES), f32),
        pltpu.VMEM((2, 3, rows), f32),
        pltpu.VMEM((2, 4, rows), f32),
        pltpu.VMEM((2, 3, rows), f32),
        pltpu.VMEM((2, 4, rows), f32),
        pltpu.VMEM((2, 3, layers, lanes), f32),
        pltpu.VMEM((2, 4, layers, lanes), f32),
        pltpu.VMEM((2, 3, layers, lanes), f32),
        pltpu.VMEM((2, 4, layers, lanes), f32),
        pltpu.SemaphoreType.DMA((2, 2, 4)),
        pltpu.SemaphoreType.DMA((2, 4, n_road - 1)),
    ]
    if in_kernel_sum:
        scratch += [
            pltpu.VMEM((n_road, n_blk) + load_shape, f32),
            pltpu.VMEM((n_road - 1, n_blk) + load_shape, f32),
            pltpu.VMEM((n_blk,) + load_shape, f32),
            pltpu.VMEM((n_blk - 1,) + load_shape, f32),
            pltpu.SemaphoreType.DMA((2, n_road - 1)),
            pltpu.SemaphoreType.DMA((2, n_blk - 1)),
        ]
    vmem = pl.BlockSpec(memory_space=pltpu.VMEM)
    hbm = pl.BlockSpec(memory_space=pl.ANY)
    smem = pl.BlockSpec(memory_space=pltpu.SMEM)
    velocity, load = pl.pallas_call(
        functools.partial(kernel, n_blk, n_road, lat, in_kernel_sum),
        out_shape=(
            pltpu.VMEM((3, rows, lanes), f32),
            pltpu.VMEM(load_shape, f32),
        ),
        in_specs=[hbm] * 8 + [smem, hbm, hbm, smem],
        out_specs=(vmem, vmem),
        scratch_shapes=scratch,
        compiler_params=pltpu.CompilerParams(collective_id=0, has_side_effects=True),
    )(
        disp.reshape(3, rows, lanes),
        veloc.reshape(3, rows, lanes),
        stiff.reshape(3, rows, lanes),
        mass.reshape(rows, lanes),
        road_height.reshape(patch_rows, LANES),
        road_slope_x.reshape(patch_rows, LANES),
        road_slope_y.reshape(patch_rows, LANES),
        road_stiff.reshape(patch_rows, LANES),
        tile_list.reshape(1, tiles_need),
        pair_node.reshape(1, pairs),
        pair_slot.reshape(1, pairs),
        pair_count.reshape(1, 1),
    )
    load = load.reshape(-1)
    if not in_kernel_sum:
        load = lax.psum_scatter(load, ("blk", "road"), scatter_dimension=0, tiled=True)
    return velocity.reshape(disp.shape), load


def solution(mesh):
    in_specs = (
        P(None, None, "road", "blk"),
        P(None, None, "road", "blk"),
        P(None, None, "road", "blk"),
        P(None, "road", "blk"),
        P("road"),
        P("road"),
        P("road"),
        P("road"),
        P("blk", "road", None),
        P("blk", "road", None),
        P("blk", "road", None),
        P("blk", "road"),
    )
    out_specs = (P(None, None, "road", "blk"), P(("blk", "road")))
    body = functools.partial(on_device, mesh.shape["blk"], mesh.shape["road"])
    return jax.shard_map(body, mesh=mesh, in_specs=in_specs, out_specs=out_specs, check_vma=False)
```

```python
import functools

import jax
import jax.numpy as jnp
from jax import lax
from jax.experimental import pallas as pl
from jax.experimental.pallas import tpu as pltpu
from jax.sharding import PartitionSpec as P

TILE = 256
LANES = 128
GROUP = 1024

hardening = 0.5
time_step = 0.25

MESH = pl.DeviceIdType.MESH
NT = (((1,), (1,)), ((), ()))


def split_two(x):
    high = x.astype(jnp.bfloat16).astype(jnp.float32)
    return high, x - high


def tension(weights, strain):
    squared = strain[0] * strain[0] + strain[1] * strain[1] + strain[2] * strain[2]
    scaled = weights * (1.0 + hardening * squared)
    return [scaled * s for s in strain]


def kernel(
    n_blk,
    n_road,
    lat,
    in_kernel_sum,
    disp_in,
    veloc_in,
    stiff_in,
    mass_in,
    height,
    slope_x,
    slope_y,
    road_stiff,
    tiles,
    nodes_in,
    slots_in,
    count,
    v_out,
    load_out,
    disp,
    veloc,
    stiff,
    mass,
    nodes,
    slots,
    in_sems,
    own_sems,
    picked_vals,
    normals,
    u1,
    v1,
    force,
    node_hot,
    facet_hot,
    facet_vals,
    facet_all,
    table,
    up_send,
    down_send,
    up_recv,
    down_recv,
    side_up_send,
    side_down_send,
    side_up_recv,
    side_down_recv,
    halo_sems,
    facet_sems,
    *reduction,
):
    b = lax.axis_index("blk")
    r = lax.axis_index("road")
    rows = disp.shape[1]
    layers = rows // lat
    groups = nodes.shape[1] // GROUP
    n_rows = table.shape[1]
    half = table.shape[1] // tiles.shape[1]
    patch_rows = height.shape[0]

    def road_peer(offset):
        return {"blk": b, "road": lax.rem(r + offset, n_road)}

    def blk_peer(offset):
        return {"blk": lax.rem(b + offset, n_blk), "road": r}

    blk_offsets = range(1, n_blk) if in_kernel_sum else sorted({1, n_blk - 1})
    barrier = pltpu.get_barrier_semaphore()
    for offset in blk_offsets:
        pl.semaphore_signal(barrier, inc=1, device_id=blk_peer(offset), device_id_type=MESH)
    for offset in range(1, n_road):
        pl.semaphore_signal(barrier, inc=1, device_id=road_peer(offset), device_id_type=MESH)

    def fill_faces(step, source):
        for c in range(3):
            turned = source[c].T
            up_send[step, c : c + 1, :] = turned[LANES - 1 : LANES, :]
            down_send[step, c : c + 1, :] = turned[0:1, :]
            side_up_send[step, c] = source[c, pl.ds(lat - 1, layers, stride=lat), :]
            side_down_send[step, c] = source[c, pl.ds(0, layers, stride=lat), :]
        if step == 0:
            down_send[step, 3:4, :] = stiff[2].T[0:1, :]
            side_down_send[step, 3] = stiff[1, pl.ds(0, layers, stride=lat), :]

    def halo_copies(step):
        plan = (
            (up_send, up_recv, blk_peer(1)),
            (down_send, down_recv, blk_peer(n_blk - 1)),
            (side_up_send, side_up_recv, road_peer(1)),
            (side_down_send, side_down_recv, road_peer(n_road - 1)),
        )
        return [
            pltpu.make_async_remote_copy(
                src_ref=src.at[step],
                dst_ref=dst.at[step],
                send_sem=halo_sems.at[step, 0, i],
                recv_sem=halo_sems.at[step, 1, i],
                device_id=peer,
                device_id_type=MESH,
            )
            for i, (src, dst, peer) in enumerate(plan)
        ]

    loads_in = [
        pltpu.make_async_copy(src, dst, in_sems.at[i])
        for i, (src, dst) in enumerate(
            (
                (disp_in, disp),
                (stiff_in, stiff),
                (nodes_in, nodes),
                (slots_in, slots),
                (mass_in, mass),
                (veloc_in, veloc),
            )
        )
    ]
    for copy in loads_in:
        copy.start()
    own = (height, slope_x, slope_y, road_stiff)
    own_copies = [
        pltpu.make_async_copy(own[a], facet_all.at[a * n_road + r], own_sems.at[a]) for a in range(4)
    ]
    for copy in own_copies:
        copy.start()
    for copy in loads_in[:2]:
        copy.wait()
    fill_faces(0, disp)
    for copy in loads_in[2:4]:
        copy.wait()

    def make_hot(g, _):
        at = pl.ds(pl.multiple_of(g * GROUP, GROUP), GROUP)
        lane = lax.broadcasted_iota(jnp.int32, (LANES, GROUP), 0)
        node_lane = nodes[:, at] & (LANES - 1)
        slot_lane = slots[:, at] & (LANES - 1)
        node_hot[g] = jnp.where(lane == node_lane, 1.0, 0.0).astype(jnp.bfloat16)
        facet_hot[g] = jnp.where(lane == slot_lane, 1.0, 0.0).astype(jnp.bfloat16)
        return 0

    lax.fori_loop(0, groups, make_hot, 0, unroll=2)

    pl.semaphore_wait(barrier, len(blk_offsets) + n_road - 1)
    halos0 = halo_copies(0)
    for copy in halos0:
        copy.start()
    facet_copies = []
    for offset in range(1, n_road):
        for a in range(4):
            copy = pltpu.make_async_remote_copy(
                src_ref=own[a],
                dst_ref=facet_all.at[a * n_road + r],
                send_sem=facet_sems.at[0, a, offset - 1],
                recv_sem=facet_sems.at[1, a, offset - 1],
                device_id=road_peer(offset),
                device_id_type=MESH,
            )
            copy.start()
            facet_copies.append(copy)
    lat_index = lax.broadcasted_iota(jnp.int32, (lat, LANES), 0)
    lane_index = lax.broadcasted_iota(jnp.int32, (lat, LANES), 1)

    def layer_rows(k):
        return pl.ds(pl.multiple_of(k * lat, lat), lat)

    def inside(source, k, above, rim):
        at = layer_rows(k)
        u = [source[c, at, :] for c in range(3)]
        if rim:
            strain = u
        else:
            below = layer_rows(k - 1)
            strain = [u[c] - source[c, below, :] for c in range(3)]
        radial = tension(stiff[0, at, :], strain)
        side = tension(stiff[1, at, :], [x - pltpu.roll(x, 1, 0) for x in u])
        around = tension(stiff[2, at, :], [x - pltpu.roll(x, 1, 1) for x in u])
        for c in range(3):
            t = jnp.where(lat_index == 0, 0.0, side[c])
            w = jnp.where(lane_index == 0, 0.0, around[c])
            force[c, at, :] = (
                (above[c] - radial[c])
                + (pltpu.roll(t, lat - 1, 0) - t)
                + (pltpu.roll(w, LANES - 1, 1) - w)
            )
        return radial

    def interior(source):
        nothing = tuple(jnp.zeros((lat, LANES), jnp.float32) for _ in range(3))

        def body(i, above):
            return tuple(inside(source, layers - 1 - i, above, False))

        above = lax.fori_loop(0, layers - 1, body, nothing, unroll=3)
        inside(source, 0, above, True)

    def rim_force(step):
        stiff_around = down_recv[0, 3:4, :]
        own_around = down_send[0, 3:4, :]
        low = tension(own_around, [down_send[step, c : c + 1, :] - up_recv[step, c : c + 1, :] for c in range(3)])
        high = tension(stiff_around, [down_recv[step, c : c + 1, :] - up_send[step, c : c + 1, :] for c in range(3)])
        place = lax.broadcasted_iota(jnp.int32, (LANES, rows), 0)
        for c in range(3):
            turned = jnp.where(place == 0, -low[c], jnp.where(place == LANES - 1, high[c], 0.0))
            force[c] = force[c] + turned.T
        first = jnp.where(r == 0, 0.0, 1.0)
        last = jnp.where(r == n_road - 1, 0.0, 1.0)
        low = tension(
            side_down_send[0, 3], [side_down_send[step, c] - first * side_up_recv[step, c] for c in range(3)]
        )
        high = tension(
            last * side_down_recv[0, 3], [side_down_recv[step, c] - side_up_send[step, c] for c in range(3)]
        )
        for c in range(3):
            at = pl.ds(0, layers, stride=lat)
            force[c, at, :] = force[c, at, :] - low[c]
            at = pl.ds(lat - 1, layers, stride=lat)
            force[c, at, :] = force[c, at, :] + high[c]

    live_count = count[0, 0]

    node_row = lax.broadcasted_iota(jnp.int32, (lat, GROUP), 0)
    facet_row = lax.broadcasted_iota(jnp.int32, (n_rows, GROUP), 0)
    slot_lane = lax.broadcasted_iota(jnp.int32, (1, GROUP), 1)

    def split_rows(arrays):
        parts = [split_two(x) for x in arrays]
        return jnp.concatenate([p[0] for p in parts] + [p[1] for p in parts], axis=0).astype(jnp.bfloat16)

    def group_at(g):
        return pl.ds(pl.multiple_of(g * GROUP, GROUP), GROUP)

    def look(table_rows, hot, mask, height_of):
        found = jnp.dot(table_rows, hot, preferred_element_type=jnp.float32)
        arrays = found.shape[0] // (2 * height_of)
        out = []
        for a in range(arrays):
            both = (
                found[a * height_of : (a + 1) * height_of]
                + found[(arrays + a) * height_of : (arrays + a + 1) * height_of]
            )
            out.append(jnp.sum(jnp.where(mask, both, 0.0), axis=0, keepdims=True))
        return out

    def outer_rows(source):
        return split_rows([source[c, rows - lat : rows, :] for c in range(3)])

    def on_nodes(g):
        return node_row == (nodes[:, group_at(g)] >> 7)

    def press(g, u, h, sx, sy, ks):
        live = slot_lane + g * GROUP < live_count
        return jnp.where(live, ks * jnp.maximum(h + sx * u[0] + sy * u[1] - u[2], 0.0), 0.0)

    def gather_force(g, on_node, sx, sy, normal, pushed):
        high, low = zip(*[split_two(x) for x in (-sx * normal, -sy * normal, normal)])
        spread = jnp.concatenate([jnp.where(on_node, x, 0.0) for x in high + low], axis=0)
        return pushed + lax.dot_general(
            spread.astype(jnp.bfloat16), node_hot[g], NT, preferred_element_type=jnp.float32
        )

    def gather_load(g, on_facet, normal, loads):
        heaped = jnp.concatenate([jnp.where(on_facet, x, 0.0) for x in split_two(normal)], axis=0)
        return loads + lax.dot_general(
            heaped.astype(jnp.bfloat16), facet_hot[g], NT, preferred_element_type=jnp.float32
        )

    def on_facets(g):
        return facet_row == (slots[:, group_at(g)] >> 7)

    def stored_facet(g, a):
        return facet_vals[g, a : a + 1, :]

    no_push = jnp.zeros((6 * lat, LANES), jnp.float32)

    def outer_sum(pushed):
        return [pushed[c * lat : (c + 1) * lat] + pushed[(3 + c) * lat : (4 + c) * lat] for c in range(3)]

    def add_outer(outer_force):
        for c in range(3):
            force[c, rows - lat : rows, :] = force[c, rows - lat : rows, :] + outer_force[c]

    interior(disp)
    first_outer = outer_rows(disp)

    def pick_first(g, _):
        for c, x in enumerate(look(first_outer, node_hot[g], on_nodes(g), lat)):
            picked_vals[g, c : c + 1, :] = x
        return 0

    lax.fori_loop(0, groups, pick_first, 0, unroll=4)

    for copy in own_copies + loads_in[4:]:
        copy.wait()
    for copy in halos0:
        copy.wait()
    rim_force(0)

    def advance(k, _):
        at = layer_rows(k)
        scale = time_step / mass[at, :]
        for c in range(3):
            v = veloc[c, at, :] + scale * force[c, at, :]
            v1[c, at, :] = v
            u1[c, at, :] = disp[c, at, :] + time_step * v
        return 0

    lax.fori_loop(0, layers - 1, advance, 0)

    for copy in facet_copies:
        copy.wait()
    for j in range(tiles.shape[1]):
        for i in range(half):
            row = tiles[0, j] * half + i
            for a in range(4):
                table[a, j * half + i : j * half + i + 1, :] = facet_all[
                    a * n_road + row // patch_rows, pl.ds(row % patch_rows, 1), :
                ]
    looked_from = split_rows([table[a] for a in range(4)])

    def first_contact(g, pushed):
        values = look(looked_from, facet_hot[g], on_facets(g), n_rows)
        for a in range(4):
            facet_vals[g, a : a + 1, :] = values[a]
        h, sx, sy, ks = values
        normal = press(g, [picked_vals[g, c : c + 1, :] for c in range(3)], h, sx, sy, ks)
        normals[g, 0:1, :] = normal
        return gather_force(g, on_nodes(g), sx, sy, normal, pushed)

    add_outer(outer_sum(lax.fori_loop(0, groups, first_contact, no_push, unroll=4)))
    advance(layers - 1, 0)

    second_outer = outer_rows(u1)

    def second_press(g, loads):
        u = look(second_outer, node_hot[g], on_nodes(g), lat)
        normal = press(g, u, *[stored_facet(g, a) for a in range(4)])
        normals[g, 1:2, :] = normal
        return gather_load(g, on_facets(g), normal + normals[g, 0:1, :], loads)

    loads = lax.fori_loop(
        0, groups, second_press, jnp.zeros((2 * n_rows, LANES), jnp.float32), unroll=4
    )
    loads = loads[:n_rows] + loads[n_rows:]

    def dense(shape, row_of):
        row = row_of(shape)
        total = jnp.zeros(shape, jnp.float32)
        for j in range(n_rows):
            here = tiles[0, j // half] * half + j % half
            line = loads[j : j + 1, :].reshape((1,) * (len(shape) - 1) + (LANES,))
            total = total + jnp.where(row == here, line, 0.0)
        return total

    if in_kernel_sum:
        spread_out, road_recv, reduced, blk_recv, road_sems, blk_sems = reduction
        chunk_rows = load_out.shape[0]
        for to in range(n_road):
            spread_out[to] = dense(
                (n_blk, chunk_rows, LANES),
                lambda s: (lax.broadcasted_iota(jnp.int32, s, 0) * n_road + to) * chunk_rows
                + lax.broadcasted_iota(jnp.int32, s, 1),
            )
        road_copies = []
        for offset in range(1, n_road):
            copy = pltpu.make_async_remote_copy(
                src_ref=spread_out.at[lax.rem(r + offset, n_road)],
                dst_ref=road_recv.at[offset - 1],
                send_sem=road_sems.at[0, offset - 1],
                recv_sem=road_sems.at[1, offset - 1],
                device_id=road_peer(offset),
                device_id_type=MESH,
            )
            copy.start()
            road_copies.append(copy)
    else:
        load_out[...] = dense(load_out.shape, lambda s: lax.broadcasted_iota(jnp.int32, s, 0))

    fill_faces(1, u1)
    halos1 = halo_copies(1)
    for copy in halos1:
        copy.start()
    interior(u1)

    if in_kernel_sum:
        for copy in road_copies:
            copy.wait()
        total = spread_out[r]
        for i in range(n_road - 1):
            total = total + road_recv[i]
        reduced[...] = total
        blk_copies = []
        for offset in range(1, n_blk):
            copy = pltpu.make_async_remote_copy(
                src_ref=reduced.at[lax.rem(b + offset, n_blk)],
                dst_ref=blk_recv.at[offset - 1],
                send_sem=blk_sems.at[0, offset - 1],
                recv_sem=blk_sems.at[1, offset - 1],
                device_id=blk_peer(offset),
                device_id_type=MESH,
            )
            copy.start()
            blk_copies.append(copy)

    def second_contact(g, pushed):
        return gather_force(
            g, on_nodes(g), stored_facet(g, 1), stored_facet(g, 2), normals[g, 1:2, :], pushed
        )

    add_outer(outer_sum(lax.fori_loop(0, groups, second_contact, no_push, unroll=4)))
    for copy in halos1:
        copy.wait()
    rim_force(1)

    def finish(k, _):
        at = layer_rows(k)
        scale = time_step / mass[at, :]
        for c in range(3):
            v_out[c, at, :] = v1[c, at, :] + scale * force[c, at, :]
        return 0

    lax.fori_loop(0, layers, finish, 0)

    if in_kernel_sum:
        for copy in blk_copies:
            copy.wait()
        total = reduced[b]
        for i in range(n_blk - 1):
            total = total + blk_recv[i]
        load_out[...] = total


def on_device(
    n_blk,
    n_road,
    disp,
    veloc,
    stiff,
    mass,
    road_height,
    road_slope_x,
    road_slope_y,
    road_stiff,
    tile_list,
    pair_node,
    pair_slot,
    pair_count,
):
    _, layers, lat, lanes = disp.shape
    rows = layers * lat
    pairs = pair_node.shape[-1]
    groups = pairs // GROUP
    tiles_need = tile_list.shape[-1]
    patch_rows = road_height.shape[0] // LANES
    total_rows = patch_rows * n_road
    table_rows = tiles_need * TILE // LANES
    devices = n_blk * n_road
    in_kernel_sum = total_rows % devices == 0
    f32 = jnp.float32
    if in_kernel_sum:
        load_shape = (total_rows // devices, LANES)
    else:
        load_shape = (total_rows, LANES)
    scratch = [
        pltpu.VMEM((3, rows, lanes), f32),
        pltpu.VMEM((3, rows, lanes), f32),
        pltpu.VMEM((3, rows, lanes), f32),
        pltpu.VMEM((rows, lanes), f32),
        pltpu.VMEM((1, pairs), jnp.int32),
        pltpu.VMEM((1, pairs), jnp.int32),
        pltpu.SemaphoreType.DMA((6,)),
        pltpu.SemaphoreType.DMA((4,)),
        pltpu.VMEM((groups, 3, GROUP), f32),
        pltpu.VMEM((groups, 2, GROUP), f32),
        pltpu.VMEM((3, rows, lanes), f32),
        pltpu.VMEM((3, rows, lanes), f32),
        pltpu.VMEM((3, rows, lanes), f32),
        pltpu.VMEM((groups, LANES, GROUP), jnp.bfloat16),
        pltpu.VMEM((groups, LANES, GROUP), jnp.bfloat16),
        pltpu.VMEM((groups, 4, GROUP), f32),
        pltpu.VMEM((4 * n_road, patch_rows, LANES), f32),
        pltpu.VMEM((4, table_rows, LANES), f32),
        pltpu.VMEM((2, 3, rows), f32),
        pltpu.VMEM((2, 4, rows), f32),
        pltpu.VMEM((2, 3, rows), f32),
        pltpu.VMEM((2, 4, rows), f32),
        pltpu.VMEM((2, 3, layers, lanes), f32),
        pltpu.VMEM((2, 4, layers, lanes), f32),
        pltpu.VMEM((2, 3, layers, lanes), f32),
        pltpu.VMEM((2, 4, layers, lanes), f32),
        pltpu.SemaphoreType.DMA((2, 2, 4)),
        pltpu.SemaphoreType.DMA((2, 4, n_road - 1)),
    ]
    if in_kernel_sum:
        scratch += [
            pltpu.VMEM((n_road, n_blk) + load_shape, f32),
            pltpu.VMEM((n_road - 1, n_blk) + load_shape, f32),
            pltpu.VMEM((n_blk,) + load_shape, f32),
            pltpu.VMEM((n_blk - 1,) + load_shape, f32),
            pltpu.SemaphoreType.DMA((2, n_road - 1)),
            pltpu.SemaphoreType.DMA((2, n_blk - 1)),
        ]
    vmem = pl.BlockSpec(memory_space=pltpu.VMEM)
    hbm = pl.BlockSpec(memory_space=pl.ANY)
    smem = pl.BlockSpec(memory_space=pltpu.SMEM)
    velocity, load = pl.pallas_call(
        functools.partial(kernel, n_blk, n_road, lat, in_kernel_sum),
        out_shape=(
            pltpu.VMEM((3, rows, lanes), f32),
            pltpu.VMEM(load_shape, f32),
        ),
        in_specs=[hbm] * 8 + [smem, hbm, hbm, smem],
        out_specs=(vmem, vmem),
        scratch_shapes=scratch,
        compiler_params=pltpu.CompilerParams(collective_id=0, has_side_effects=True),
    )(
        disp.reshape(3, rows, lanes),
        veloc.reshape(3, rows, lanes),
        stiff.reshape(3, rows, lanes),
        mass.reshape(rows, lanes),
        road_height.reshape(patch_rows, LANES),
        road_slope_x.reshape(patch_rows, LANES),
        road_slope_y.reshape(patch_rows, LANES),
        road_stiff.reshape(patch_rows, LANES),
        tile_list.reshape(1, tiles_need),
        pair_node.reshape(1, pairs),
        pair_slot.reshape(1, pairs),
        pair_count.reshape(1, 1),
    )
    load = load.reshape(-1)
    if not in_kernel_sum:
        load = lax.psum_scatter(load, ("blk", "road"), scatter_dimension=0, tiled=True)
    return velocity.reshape(disp.shape), load


def solution(mesh):
    in_specs = (
        P(None, None, "road", "blk"),
        P(None, None, "road", "blk"),
        P(None, None, "road", "blk"),
        P(None, "road", "blk"),
        P("road"),
        P("road"),
        P("road"),
        P("road"),
        P("blk", "road", None),
        P("blk", "road", None),
        P("blk", "road", None),
        P("blk", "road"),
    )
    out_specs = (P(None, None, "road", "blk"), P(("blk", "road")))
    body = functools.partial(on_device, mesh.shape["blk"], mesh.shape["road"])
    return jax.shard_map(body, mesh=mesh, in_specs=in_specs, out_specs=out_specs, check_vma=False)
```
